32 devices in a mesh: pat: 8 (over z, core), pb: 4 (over y, x).
Axes of the slice: x: 2, y: 2, z: 4, core: 2. Of those that a mesh axis runs over, the one named last changes fastest.
Arguments:
- measured: float32 [16384, 4096], P(('pat', 'pb')), may hold values from 1 to 10
- resolution: float32 [33, 4096], replicated, may hold values from 0.05 to 1
- loadings_start: float32 [16384, 128], P('pat'), may hold values from 0.05 to 0.5
- components_start: float32 [128, 4096], P(None, 'pb'), may hold values from 0.05 to 0.5
Outputs:
- loadings: float32 [16384, 128], P('pat')
- components: float32 [128, 4096], P(None, 'pb')
The draws below stay inside these ranges and needn't reach their ends.
All inputs are finite; a program needn't handle non-finite values.
Results may differ from the reference program's by a relative error of at most 0.00013.
Values sent between devices are 32-bit elements; how exact they have to be, the bound alone decides.
A program may use at most 384 MiB of HBM per device.

```python
import math
import jax
import jax.numpy as jnp
from jax import lax

Q = 4096
COMPONENTS = 128
RADIUS = 16
TAPS = 33
ITERS = 3
PATTERNS = 16384


def steps_of(own_key, dims, split, least, high):
    def one(position, parts):
        heights = jax.random.uniform(jax.random.fold_in(jax.random.fold_in(own_key, 6), position), (parts,), jnp.float32, least / len(split), high / len(split))
        return jnp.repeat(jnp.exp(heights), dims[position] // parts).reshape((-1,) + (1,) * (len(dims) - position - 1))

    loudness = one(*split[0])
    for cut in split[1:]:
        loudness = loudness * one(*cut)
    return loudness


def setup_inputs(seed: int = 0) -> dict:
    arg_keys = jax.random.split(jax.random.key(seed), 5)
    return {
        "measured": jnp.clip(jnp.exp(math.log(10.0) - 2.3025851 * jax.random.uniform(arg_keys[0], (PATTERNS, Q), jnp.float32) ** steps_of(arg_keys[0], (PATTERNS, Q), ((0, 32),), -0.2, 0.2)), 1.0, 10.0),
        "resolution": jnp.clip(jnp.exp(jax.random.uniform(arg_keys[1], (TAPS, Q), jnp.float32, math.log(0.05), math.log(1.0))), 0.05, 1.0),
        "loadings_start": jnp.clip(jnp.exp(math.log(0.5) - 2.3025851 * jax.random.uniform(arg_keys[2], (PATTERNS, COMPONENTS), jnp.float32) ** steps_of(arg_keys[2], (PATTERNS, COMPONENTS), ((0, 8),), -0.2, 0.2)), 0.05, 0.5),
        "components_start": jnp.clip(jnp.exp(math.log(0.5) - 2.3025851 * jax.random.uniform(arg_keys[3], (COMPONENTS, Q), jnp.float32) ** steps_of(arg_keys[3], (COMPONENTS, Q), ((1, 4),), -0.2, 0.2)), 0.05, 0.5),
    }


def smear_forward(field, resolution):
    width = field.shape[1]
    padded = jnp.pad(field, ((0, 0), (RADIUS, RADIUS)))
    total = jnp.zeros(field.shape, jnp.float32)
    for offset in range(2 * RADIUS + 1):
        total = total + resolution[offset][None, :] * padded[:, offset:offset + width]
    return total


def smear_back(field, resolution):
    width = field.shape[1]
    total = jnp.zeros(field.shape, jnp.float32)
    for offset in range(2 * RADIUS + 1):
        weighted = jnp.pad(resolution[offset][None, :] * field, ((0, 0), (RADIUS, RADIUS)))
        begin = 2 * RADIUS - offset
        total = total + weighted[:, begin:begin + width]
    return total


def correct_block(measured, resolution):
    blurred = smear_forward(measured, resolution)
    back = smear_back(measured / blurred, resolution)
    weight_sum = smear_back(jnp.ones((1, measured.shape[1]), jnp.float32), resolution)
    return measured * back / weight_sum


def reference(measured, resolution, loadings_start, components_start):
    rows = measured.shape[0]
    block = min(rows, 1024)
    stacked = measured.reshape(rows // block, block, measured.shape[1])
    corrected = lax.map(lambda piece: correct_block(piece, resolution), stacked).reshape(measured.shape)
    loadings = loadings_start
    components = components_start
    high = lax.Precision.HIGHEST
    for step in range(ITERS):
        quotient = corrected / jnp.dot(loadings, components, precision=high)
        numerator = jnp.dot(loadings.T, quotient, precision=high)
        w_totals = jnp.sum(loadings, axis=0)
        components = components * numerator / w_totals[:, None]
        quotient = corrected / jnp.dot(loadings, components, precision=high)
        numerator = jnp.dot(quotient, components.T, precision=high)
        h_totals = jnp.sum(components, axis=1)
        loadings = loadings * numerator / h_totals[None, :]
    return loadings, components
```

```python
import jax
import jax.numpy as jnp
from jax import lax
from jax.experimental import pallas as pl
from jax.experimental.pallas import tpu as pltpu
from jax.sharding import PartitionSpec as P

ITERS = 3
LANES = 128
BAND = 256
AXES = ("pat", "pb")


def split(x):
    high = x.astype(jnp.bfloat16)
    return high, (x - high.astype(jnp.float32)).astype(jnp.bfloat16)


def dot(a, b):
    return jnp.dot(a, b, preferred_element_type=jnp.float32)


def dot_nt(a, b):
    return lax.dot_general(
        a, b, (((1,), (1,)), ((), ())), preferred_element_type=jnp.float32
    )


def smear_kernel(taps, v_ref, r_ref, out_ref, bh, bl, vh, vl, acc, wacc):
    rows, width = v_ref.shape
    blocks = width // BAND
    radius = taps // 2
    window = BAND + 2 * LANES

    @pl.when(pl.program_id(0) == 0)
    def _():
        wacc[...] = jnp.zeros_like(wacc)

        @pl.loop(0, blocks)
        def _(j):
            at = pl.multiple_of(j * BAND, BAND)
            weights = r_ref[pl.ds(at, BAND), :]
            wide = jnp.concatenate(
                [weights, jnp.zeros((BAND, window - LANES), jnp.float32)], axis=1
            )
            band = pltpu.roll(wide, LANES - radius, 1, stride=1, stride_axis=0)
            bh[j], bl[j] = split(band)
            wacc[:, pl.ds(at, window)] += jnp.broadcast_to(
                jnp.sum(band, axis=0, keepdims=True), (8, window)
            )

    edge = jnp.zeros((rows, LANES), jnp.bfloat16)
    for ref in (vh, vl):
        ref[:, :LANES] = edge
        ref[:, width + LANES :] = edge

    @pl.loop(0, blocks)
    def _(j):
        at = pl.multiple_of(j * BAND, BAND)
        high, low = split(v_ref[:, pl.ds(at, BAND)])
        vh[:, pl.ds(at + LANES, BAND)] = high
        vl[:, pl.ds(at + LANES, BAND)] = low
        acc[:, pl.ds(at, BAND)] = jnp.zeros((rows, BAND), jnp.float32)

    acc[:, width:] = jnp.zeros((rows, 2 * LANES), jnp.float32)

    @pl.loop(0, blocks)
    def _(j):
        at = pl.multiple_of(j * BAND, BAND)
        kh, kl = bh[j], bl[j]
        xh = vh[:, pl.ds(at, window)]
        blurred = dot_nt(xh, kh) + dot_nt(xh, kl) + dot_nt(vl[:, pl.ds(at, window)], kh)
        uh, ul = split(v_ref[:, pl.ds(at, BAND)] / blurred)
        acc[:, pl.ds(at, window)] += dot(uh, kh) + dot(uh, kl) + dot(ul, kh)

    @pl.loop(0, blocks)
    def _(j):
        at = pl.multiple_of(j * BAND, BAND)
        here = pl.ds(at + LANES, BAND)
        out_ref[:, pl.ds(at, BAND)] = (
            v_ref[:, pl.ds(at, BAND)] * acc[:, here] / wacc[:1, here]
        )


def correct(measured, resolution):
    total, width = measured.shape
    taps = resolution.shape[0]
    rows = min(total, 256)
    weights = jnp.pad(resolution.T, ((0, 0), (0, LANES - taps)))
    blocks = width // BAND
    window = BAND + 2 * LANES
    padded = width + 2 * LANES

    def body(*refs):
        smear_kernel(taps, *refs)

    return pl.pallas_call(
        body,
        grid=(total // rows,),
        out_shape=jax.ShapeDtypeStruct(measured.shape, jnp.float32),
        in_specs=[
            pl.BlockSpec((rows, width), lambda i: (i, 0)),
            pl.BlockSpec((width, LANES), lambda i: (0, 0)),
        ],
        out_specs=pl.BlockSpec((rows, width), lambda i: (i, 0)),
        scratch_shapes=[
            pltpu.VMEM((blocks, BAND, window), jnp.bfloat16),
            pltpu.VMEM((blocks, BAND, window), jnp.bfloat16),
            pltpu.VMEM((rows, padded), jnp.bfloat16),
            pltpu.VMEM((rows, padded), jnp.bfloat16),
            pltpu.VMEM((rows, padded), jnp.float32),
            pltpu.VMEM((8, padded), jnp.float32),
        ],
        cost_estimate=pl.CostEstimate(
            flops=12 * total * width * window, bytes_accessed=8 * total * width,
            transcendentals=0,
        ),
        name="smear",
    )(measured, weights)


def quotient_of(x_ref, l, c_ref):
    c = jnp.concatenate([c_ref[i] for i in range(c_ref.shape[0])], axis=1)
    lh, ll = split(l)
    ch, cl = split(c)
    model = dot(
        jnp.concatenate([lh, ll, lh], axis=1), jnp.concatenate([ch, ch, cl], axis=0)
    )
    qh, ql = split(x_ref[...] / model)
    return qh, ql, ch, cl


def numer_kernel(x_ref, l_ref, lt_ref, c_ref, out_ref):
    comps = l_ref.shape[1]
    l = l_ref[...]
    qh, ql, _, _ = quotient_of(x_ref, l, c_ref)
    th, tl = split(lt_ref[...])
    both = dot(jnp.concatenate([th, tl], axis=0), qh)
    numer = both[:comps] + both[comps:] + dot(th, ql)
    totals = jnp.broadcast_to(jnp.sum(l, axis=0, keepdims=True), (8, comps))
    for i in range(c_ref.shape[0]):
        out_ref[i, :comps, :] = numer[:, i * LANES : (i + 1) * LANES]
        out_ref[i, comps:, :] = totals


def load_kernel(x_ref, l_ref, c_ref, l_out, lt_out, acc, sums):
    comps = l_ref.shape[1]
    step = pl.program_id(0)

    @pl.when(step == 0)
    def _():
        acc[...] = jnp.zeros_like(acc)
        sums[...] = jnp.zeros_like(sums)

    l = l_ref[...]
    qh, ql, ch, cl = quotient_of(x_ref, l, c_ref)
    both = dot_nt(qh, jnp.concatenate([ch, cl], axis=0))
    acc[...] += both[:, :comps] + both[:, comps:] + dot_nt(ql, ch)
    here = c_ref[0]
    for i in range(1, c_ref.shape[0]):
        here = here + c_ref[i]
    sums[...] += here

    @pl.when(step == pl.num_programs(0) - 1)
    def _():
        totals = jnp.sum(sums[...].T, axis=0, keepdims=True)
        new = l * acc[...] / totals
        l_out[...] = new
        lt_out[...] = new.T


def cost(x, comps):
    return pl.CostEstimate(
        flops=12 * x.size * comps, bytes_accessed=4 * x.size, transcendentals=0
    )


STEP = 512


def numerators(x, l, lt, c):
    rows, width = x.shape
    comps = l.shape[1]
    per = STEP // LANES
    return pl.pallas_call(
        numer_kernel,
        grid=(width // STEP,),
        out_shape=jax.ShapeDtypeStruct((width // LANES, comps + 8, LANES), jnp.float32),
        in_specs=[
            pl.BlockSpec((rows, STEP), lambda i: (0, i)),
            pl.BlockSpec((rows, comps), lambda i: (0, 0)),
            pl.BlockSpec((comps, rows), lambda i: (0, 0)),
            pl.BlockSpec((per, comps, LANES), lambda i: (i, 0, 0)),
        ],
        out_specs=pl.BlockSpec((per, comps + 8, LANES), lambda i: (i, 0, 0)),
        cost_estimate=cost(x, comps),
        name="numer",
    )(x, l, lt, c)


def new_loadings(x, l, c):
    rows, width = x.shape
    comps = l.shape[1]
    per = STEP // LANES
    return pl.pallas_call(
        load_kernel,
        grid=(width // STEP,),
        out_shape=(
            jax.ShapeDtypeStruct((rows, comps), jnp.float32),
            jax.ShapeDtypeStruct((comps, rows), jnp.float32),
        ),
        in_specs=[
            pl.BlockSpec((rows, STEP), lambda i: (0, i)),
            pl.BlockSpec((rows, comps), lambda i: (0, 0)),
            pl.BlockSpec((per, comps, LANES), lambda i: (i, 0, 0)),
        ],
        out_specs=(
            pl.BlockSpec((rows, comps), lambda i: (0, 0)),
            pl.BlockSpec((comps, rows), lambda i: (0, 0)),
        ),
        scratch_shapes=[
            pltpu.VMEM((rows, comps), jnp.float32),
            pltpu.VMEM((comps, LANES), jnp.float32),
        ],
        cost_estimate=cost(x, comps),
        name="loads",
    )(x, l, c)


def regroup(blocks, count):
    if blocks.shape[0] == count:
        return blocks
    comps = blocks.shape[1]
    flat = jnp.swapaxes(blocks, 0, 1).reshape(comps, -1)
    return jnp.swapaxes(flat.reshape(comps, count, -1), 0, 1)


def scatter(num):
    blocks, height, cols = num.shape
    flat = num.reshape(blocks * height, cols)
    flat = lax.psum_scatter(flat, "pat", scatter_dimension=0, tiled=True)
    flat = lax.psum_scatter(flat, "pb", scatter_dimension=0, tiled=True)
    return flat.reshape(1, height, cols)


def local(devices, measured, resolution, loadings_start, components_start):
    rows, width = measured.shape
    comps = loadings_start.shape[1]
    cols = width // devices
    lane_blocks = width // LANES
    first_row = lax.axis_index("pb") * rows
    l = lax.dynamic_slice_in_dim(loadings_start, first_row, rows, 0)
    lt = l.T
    start = regroup(components_start[None], components_start.shape[1] // LANES)
    c = lax.all_gather(start, "pb", axis=0, tiled=True)
    own = lax.dynamic_slice_in_dim(
        regroup(c, devices), lax.axis_index(AXES), 1, 0
    )
    x = correct(measured, resolution)
    for step in range(ITERS):
        num = numerators(x, l, lt, c)
        if cols != LANES:
            extra = -(-comps // cols)
            totals = jnp.pad(num[0, comps], (0, extra * cols - comps))
            totals = jnp.broadcast_to(
                totals.reshape(1, extra, cols), (devices, extra, cols)
            )
            num = jnp.concatenate([regroup(num[:, :comps], devices), totals], axis=1)
        share = scatter(num)
        totals = share[0, comps:].reshape(-1)[:comps]
        own = own * share[:, :comps] / totals[None, :, None]
        c = regroup(lax.all_gather(own, AXES, axis=0, tiled=True), lane_blocks)
        l, lt = new_loadings(x, l, c)
    loadings = lax.all_gather(l, "pb", axis=0, tiled=True)
    count = components_start.shape[1] // LANES
    mine = lax.dynamic_slice_in_dim(c, lax.axis_index("pb") * count, count, 0)
    return loadings, jnp.swapaxes(mine, 0, 1).reshape(comps, -1)


def solution(mesh):
    devices = mesh.shape["pat"] * mesh.shape["pb"]

    def body(*args):
        return local(devices, *args)

    return jax.shard_map(
        body,
        mesh=mesh,
        in_specs=(P(("pat", "pb"), None), P(), P("pat", None), P(None, "pb")),
        out_specs=(P("pat", None), P(None, "pb")),
        check_vma=False,
    )
```

```python
import jax
import jax.numpy as jnp
from jax import lax
from jax.experimental import pallas as pl
from jax.experimental.pallas import tpu as pltpu
from jax.sharding import PartitionSpec as P

ITERS = 3
LANES = 128
BAND = 256
AXES = ("pat", "pb")


def split(x):
    high = x.astype(jnp.bfloat16)
    return high, (x - high.astype(jnp.float32)).astype(jnp.bfloat16)


def dot(a, b):
    return jnp.dot(a, b, preferred_element_type=jnp.float32)


def dot_nt(a, b):
    return lax.dot_general(
        a, b, (((1,), (1,)), ((), ())), preferred_element_type=jnp.float32
    )


def smear_kernel(taps, v_ref, r_ref, out_ref, bh, bl, vh, vl, acc, wacc):
    rows, width = v_ref.shape
    blocks = width // BAND
    radius = taps // 2
    window = BAND + 2 * LANES

    @pl.when(pl.program_id(0) == 0)
    def _():
        wacc[...] = jnp.zeros_like(wacc)

        @pl.loop(0, blocks)
        def _(j):
            at = pl.multiple_of(j * BAND, BAND)
            weights = r_ref[pl.ds(at, BAND), :]
            wide = jnp.concatenate(
                [weights, jnp.zeros((BAND, window - LANES), jnp.float32)], axis=1
            )
            band = pltpu.roll(wide, LANES - radius, 1, stride=1, stride_axis=0)
            bh[j], bl[j] = split(band)
            wacc[:, pl.ds(at, window)] += jnp.broadcast_to(
                jnp.sum(band, axis=0, keepdims=True), (8, window)
            )

    edge = jnp.zeros((rows, LANES), jnp.bfloat16)
    for ref in (vh, vl):
        ref[:, :LANES] = edge
        ref[:, width + LANES :] = edge

    @pl.loop(0, blocks)
    def _(j):
        at = pl.multiple_of(j * BAND, BAND)
        high, low = split(v_ref[:, pl.ds(at, BAND)])
        vh[:, pl.ds(at + LANES, BAND)] = high
        vl[:, pl.ds(at + LANES, BAND)] = low
        acc[:, pl.ds(at, BAND)] = jnp.zeros((rows, BAND), jnp.float32)

    acc[:, width:] = jnp.zeros((rows, 2 * LANES), jnp.float32)

    @pl.loop(0, blocks)
    def _(j):
        at = pl.multiple_of(j * BAND, BAND)
        kh, kl = bh[j], bl[j]
        xh = vh[:, pl.ds(at, window)]
        blurred = dot_nt(xh, kh) + dot_nt(xh, kl) + dot_nt(vl[:, pl.ds(at, window)], kh)
        uh, ul = split(v_ref[:, pl.ds(at, BAND)] / blurred)
        acc[:, pl.ds(at, window)] += dot(uh, kh) + dot(uh, kl) + dot(ul, kh)

    @pl.loop(0, blocks)
    def _(j):
        at = pl.multiple_of(j * BAND, BAND)
        here = pl.ds(at + LANES, BAND)
        out_ref[:, pl.ds(at, BAND)] = (
            v_ref[:, pl.ds(at, BAND)] * acc[:, here] / wacc[:1, here]
        )


def correct(measured, resolution):
    total, width = measured.shape
    taps = resolution.shape[0]
    rows = min(total, 256)
    weights = jnp.pad(resolution.T, ((0, 0), (0, LANES - taps)))
    blocks = width // BAND
    window = BAND + 2 * LANES
    padded = width + 2 * LANES

    def body(*refs):
        smear_kernel(taps, *refs)

    return pl.pallas_call(
        body,
        grid=(total // rows,),
        out_shape=jax.ShapeDtypeStruct(measured.shape, jnp.float32),
        in_specs=[
            pl.BlockSpec((rows, width), lambda i: (i, 0)),
            pl.BlockSpec((width, LANES), lambda i: (0, 0)),
        ],
        out_specs=pl.BlockSpec((rows, width), lambda i: (i, 0)),
        scratch_shapes=[
            pltpu.VMEM((blocks, BAND, window), jnp.bfloat16),
            pltpu.VMEM((blocks, BAND, window), jnp.bfloat16),
            pltpu.VMEM((rows, padded), jnp.bfloat16),
            pltpu.VMEM((rows, padded), jnp.bfloat16),
            pltpu.VMEM((rows, padded), jnp.float32),
            pltpu.VMEM((8, padded), jnp.float32),
        ],
        cost_estimate=pl.CostEstimate(
            flops=12 * total * width * window, bytes_accessed=8 * total * width,
            transcendentals=0,
        ),
        name="smear",
    )(measured, weights)


def quotient_of(x_ref, l, c_ref):
    c = jnp.concatenate([c_ref[i] for i in range(c_ref.shape[0])], axis=1)
    lh, ll = split(l)
    ch, cl = split(c)
    model = dot(
        jnp.concatenate([lh, ll, lh], axis=1), jnp.concatenate([ch, ch, cl], axis=0)
    )
    qh, ql = split(x_ref[...] / model)
    return qh, ql, ch, cl


def numer_kernel(x_ref, l_ref, lt_ref, c_ref, out_ref):
    comps = l_ref.shape[1]
    l = l_ref[...]
    qh, ql, _, _ = quotient_of(x_ref, l, c_ref)
    th, tl = split(lt_ref[...])
    both = dot(jnp.concatenate([th, tl], axis=0), qh)
    numer = both[:comps] + both[comps:] + dot(th, ql)
    totals = jnp.broadcast_to(jnp.sum(l, axis=0, keepdims=True), (8, comps))
    for i in range(c_ref.shape[0]):
        out_ref[i, :comps, :] = numer[:, i * LANES : (i + 1) * LANES]
        out_ref[i, comps:, :] = totals


def load_kernel(x_ref, l_ref, c_ref, l_out, lt_out, acc, sums):
    comps = l_ref.shape[1]
    step = pl.program_id(0)

    @pl.when(step == 0)
    def _():
        acc[...] = jnp.zeros_like(acc)
        sums[...] = jnp.zeros_like(sums)

    l = l_ref[...]
    qh, ql, ch, cl = quotient_of(x_ref, l, c_ref)
    both = dot_nt(qh, jnp.concatenate([ch, cl], axis=0))
    acc[...] += both[:, :comps] + both[:, comps:] + dot_nt(ql, ch)
    here = c_ref[0]
    for i in range(1, c_ref.shape[0]):
        here = here + c_ref[i]
    sums[...] += here

    @pl.when(step == pl.num_programs(0) - 1)
    def _():
        totals = jnp.sum(sums[...].T, axis=0, keepdims=True)
        new = l * acc[...] / totals
        l_out[...] = new
        lt_out[...] = new.T


def cost(x, comps):
    return pl.CostEstimate(
        flops=12 * x.size * comps, bytes_accessed=4 * x.size, transcendentals=0
    )


STEP = 512


def numerators(x, l, lt, c):
    rows, width = x.shape
    comps = l.shape[1]
    per = STEP // LANES
    return pl.pallas_call(
        numer_kernel,
        grid=(width // STEP,),
        out_shape=jax.ShapeDtypeStruct((width // LANES, comps + 8, LANES), jnp.float32),
        in_specs=[
            pl.BlockSpec((rows, STEP), lambda i: (0, i)),
            pl.BlockSpec((rows, comps), lambda i: (0, 0)),
            pl.BlockSpec((comps, rows), lambda i: (0, 0)),
            pl.BlockSpec((per, comps, LANES), lambda i: (i, 0, 0)),
        ],
        out_specs=pl.BlockSpec((per, comps + 8, LANES), lambda i: (i, 0, 0)),
        cost_estimate=cost(x, comps),
        name="numer",
    )(x, l, lt, c)


def new_loadings(x, l, c):
    rows, width = x.shape
    comps = l.shape[1]
    per = STEP // LANES
    return pl.pallas_call(
        load_kernel,
        grid=(width // STEP,),
        out_shape=(
            jax.ShapeDtypeStruct((rows, comps), jnp.float32),
            jax.ShapeDtypeStruct((comps, rows), jnp.float32),
        ),
        in_specs=[
            pl.BlockSpec((rows, STEP), lambda i: (0, i)),
            pl.BlockSpec((rows, comps), lambda i: (0, 0)),
            pl.BlockSpec((per, comps, LANES), lambda i: (i, 0, 0)),
        ],
        out_specs=(
            pl.BlockSpec((rows, comps), lambda i: (0, 0)),
            pl.BlockSpec((comps, rows), lambda i: (0, 0)),
        ),
        scratch_shapes=[
            pltpu.VMEM((rows, comps), jnp.float32),
            pltpu.VMEM((comps, LANES), jnp.float32),
        ],
        cost_estimate=cost(x, comps),
        name="loads",
    )(x, l, c)


def regroup(blocks, count):
    if blocks.shape[0] == count:
        return blocks
    comps = blocks.shape[1]
    flat = jnp.swapaxes(blocks, 0, 1).reshape(comps, -1)
    return jnp.swapaxes(flat.reshape(comps, count, -1), 0, 1)


def scatter(num):
    blocks, height, cols = num.shape
    flat = num.reshape(blocks * height, cols)
    flat = lax.psum_scatter(flat, "pat", scatter_dimension=0, tiled=True)
    flat = lax.psum_scatter(flat, "pb", scatter_dimension=0, tiled=True)
    return flat.reshape(1, height, cols)


MESH = pl.DeviceIdType.MESH


def bits_of(pat, pb):
    count = pat.bit_length() - 1, pb.bit_length() - 1
    return (
        [("pat", 0)]
        + [("pb", i) for i in range(count[1])]
        + [("pat", i) for i in range(1, count[0])]
    )


def orders_of(bits):
    ahead = list(range(len(bits)))
    other = list(ahead)
    other[1], other[2] = 2, 1
    return ahead, other


def my_bit(bit):
    return lax.rem(lax.axis_index(bit[0]) // (1 << bit[1]), 2)


def exchange_kernel(bits, groups, comps, num_ref, own_ref, c_ref, new_ref, *scratch):
    dims = len(bits)
    mine = [my_bit(b) for b in bits]
    place = {"pat": lax.axis_index("pat"), "pb": lax.axis_index("pb")}
    peers = []
    for (axis, i), bit in zip(bits, mine):
        moved = place[axis] + (1 - 2 * bit) * (1 << i)
        peers.append(
            (moved, place["pb"]) if axis == "pat" else (place["pat"], moved)
        )
    count = len(groups)
    bufs = [scratch[g * dims : (g + 1) * dims] for g in range(count)]
    send, recv = scratch[count * dims :]

    barrier = pltpu.get_barrier_semaphore()
    for peer in peers:
        pl.semaphore_signal(barrier, inc=1, device_id=peer, device_id_type=MESH)
    pl.semaphore_wait(barrier, dims)

    def remote(src, dst, g, phase, k, d):
        return pltpu.make_async_remote_copy(
            src_ref=src,
            dst_ref=dst,
            send_sem=send.at[g, phase, k],
            recv_sem=recv.at[g, phase, k],
            device_id=peers[d],
            device_id_type=MESH,
        )

    def pick(g, k, side):
        order, first, size = groups[g]
        left = [d for d in range(dims) if d not in order[:k]]
        index = [slice(None)] * len(left)
        index[left.index(order[k])] = side
        if k == 0:
            return num_ref, tuple(index) + (pl.ds(first, size),)
        return bufs[g][k - 1], tuple(index)

    flying = [None] * count
    for k in range(dims + 1):
        for g in range(count):
            if k:
                flying[g].wait()
                ref, index = pick(g, k - 1, mine[groups[g][0][k - 1]])
                bufs[g][k - 1][...] += ref[index]
            if k < dims:
                d = groups[g][0][k]
                ref, index = pick(g, k, 1 - mine[d])
                flying[g] = remote(ref.at[index], bufs[g][k], g, 0, k, d)
                flying[g].start()

    sums = jnp.concatenate([bufs[g][dims - 1][...] for g in range(count)], axis=0)
    totals = jnp.broadcast_to(sums[comps : comps + 1], (LANES, comps)).T
    new = own_ref[...] * sums[:comps] / totals
    new_ref[...] = new
    c_ref[tuple(mine)] = new

    for k in range(dims + 1):
        for g in range(count):
            order, first, size = groups[g]
            if k:
                flying[g].wait()
            if k < dims:
                d = order[dims - 1 - k]
                done = order[dims - k :]
                index = tuple(slice(None) if e in done else mine[e] for e in range(dims))
                size = min(size, comps - first)
                view = c_ref.at[index + (pl.ds(first, size),)]
                flying[g] = remote(view, view, g, 1, k, d)
                flying[g].start()


def exchange(bits, num, own):
    blocks, height, cols = num.shape
    comps = own.shape[0]
    dims = len(bits)
    cut = comps // 2
    groups = [
        (order, first, size)
        for order, first, size in zip(orders_of(bits), (0, cut), (cut, height - cut))
    ]
    shape = (2,) * dims

    def body(*refs):
        exchange_kernel(bits, groups, comps, *refs)

    vmem = pl.BlockSpec(memory_space=pltpu.VMEM)
    c, new = pl.pallas_call(
        body,
        out_shape=(
            jax.ShapeDtypeStruct(shape + (comps, cols), jnp.float32),
            jax.ShapeDtypeStruct((comps, cols), jnp.float32),
        ),
        in_specs=[vmem, vmem],
        out_specs=(vmem, vmem),
        scratch_shapes=[
            pltpu.VMEM((2,) * (dims - 1 - k) + (size, cols), jnp.float32)
            for _, _, size in groups
            for k in range(dims)
        ]
        + [pltpu.SemaphoreType.DMA((len(groups), 2, dims))] * 2,
        compiler_params=pltpu.CompilerParams(collective_id=0, has_side_effects=True),
        name="exchange",
    )(num.reshape(shape + (height, cols)), own)
    return c.reshape(blocks, comps, cols), new


def local(sizes, measured, resolution, loadings_start, components_start):
    rows, width = measured.shape
    comps = loadings_start.shape[1]
    devices = sizes[0] * sizes[1]
    cols = width // devices
    lane_blocks = width // LANES
    first_row = lax.axis_index("pb") * rows
    l = lax.dynamic_slice_in_dim(loadings_start, first_row, rows, 0)
    lt = l.T
    start = regroup(components_start[None], components_start.shape[1] // LANES)
    c = lax.all_gather(start, "pb", axis=0, tiled=True)
    bits = bits_of(*sizes)
    paired = cols == LANES == comps and 1 << len(bits) == devices and sizes[1] >= 4
    position = lax.axis_index(AXES)
    if paired:
        position = 0
        for bit in bits:
            position = 2 * position + my_bit(bit)
    own = lax.dynamic_slice_in_dim(regroup(c, devices), position, 1, 0)
    x = correct(measured, resolution)
    for step in range(ITERS):
        num = numerators(x, l, lt, c)
        if paired:
            c, new = exchange(bits, num, own[0])
            own = new[None]
            l, lt = new_loadings(x, l, c)
            continue
        if cols != LANES:
            extra = -(-comps // cols)
            totals = jnp.pad(num[0, comps], (0, extra * cols - comps))
            totals = jnp.broadcast_to(
                totals.reshape(1, extra, cols), (devices, extra, cols)
            )
            num = jnp.concatenate([regroup(num[:, :comps], devices), totals], axis=1)
        share = scatter(num)
        totals = share[0, comps:].reshape(-1)[:comps]
        own = own * share[:, :comps] / totals[None, :, None]
        c = regroup(lax.all_gather(own, AXES, axis=0, tiled=True), lane_blocks)
        l, lt = new_loadings(x, l, c)
    loadings = lax.all_gather(l, "pb", axis=0, tiled=True)
    count = components_start.shape[1] // LANES
    mine = lax.dynamic_slice_in_dim(c, lax.axis_index("pb") * count, count, 0)
    return loadings, jnp.swapaxes(mine, 0, 1).reshape(comps, -1)


def solution(mesh):
    sizes = mesh.shape["pat"], mesh.shape["pb"]

    def body(*args):
        return local(sizes, *args)

    return jax.shard_map(
        body,
        mesh=mesh,
        in_specs=(P(("pat", "pb"), None), P(), P("pat", None), P(None, "pb")),
        out_specs=(P("pat", None), P(None, "pb")),
        check_vma=False,
    )
```
